32 devices in a mesh: slab: 16 (over z, y, core), amp: 2 (over x).
Axes of the slice: x: 2, y: 2, z: 4, core: 2. Of those that a mesh axis runs over, the one named last changes fastest.
Arguments:
- amplitudes: bfloat16 [409600, 704], P('slab', 'amp'), may hold values from -6 to 6
- integrals: bfloat16 [409600, 1280], P(('slab', 'amp')), may hold values from -0.0546875 to 0.0546875
- virt_irrep: int32 [640], replicated, may hold values from 0 to 7
- occ_irrep: int32 [64], replicated, may hold values from 0 to 7
Outputs:
- ladder_residual: float32 [704, 1280], P('amp', 'slab')
The draws below stay inside these ranges and needn't reach their ends.
All inputs are finite; a program needn't handle non-finite values.
Results may differ from the reference program's by a relative error of at most 0.0003.
Values may be sent and summed in bfloat16 or wider, within the bound.
A program may use at most 128 MiB of HBM per device.

```python
import jax
import jax.numpy as jnp
from jax import lax

O = 64
V = 640
IRREPS = 8
A_WIN = 2
I_WIN = 11
IJ = 704
AB = 1280
CD = 409600


def with_ends(array, rng, smallest, largest):
    longest = array.shape.index(max(array.shape))
    spots = []
    for shift in (0, 1):
        where = [jax.random.randint(jax.random.fold_in(rng, axis), (), 0, length) for axis, length in enumerate(array.shape)]
        where[longest] = (where[longest] + shift) % array.shape[longest]
        spots.append(tuple(where))
    return array.at[spots[0]].set(smallest).at[spots[1]].set(largest)


def raised(array, own_key, source, target, shards_of, factor):
    owner, partner = [(jnp.arange(array.shape[position]) // (array.shape[position] // shards_of)).reshape([-1 if axis == position else 1 for axis in range(array.ndim)]) for position in (source, target)]
    chosen = jax.random.permutation(own_key, shards_of)[partner]
    strong = (owner == chosen) | (owner == (partner + shards_of // 2) % shards_of)
    return jnp.where(strong, factor * array, array)


def levels(rng, extent, pieces, smallest, high):
    def one(dim, shards_of):
        steps = jax.random.uniform(jax.random.fold_in(jax.random.fold_in(rng, 6), dim), (shards_of,), jnp.float32, smallest / len(pieces), high / len(pieces))
        return jnp.repeat(jnp.exp(steps), extent[dim] // shards_of).reshape((-1,) + (1,) * (len(extent) - dim - 1))

    level = one(*pieces[0])
    for cut in pieces[1:]:
        level = level * one(*cut)
    return level


def gaussian_with(stream_key, shape, width, bound, cuts, heavy, held_as=jnp.bfloat16):
    result = width * jax.random.normal(stream_key, shape, jnp.float32)
    if cuts:
        result = result * levels(stream_key, shape, cuts, -0.22, 0.18)
    return jnp.clip(raised(result, jax.random.fold_in(stream_key, 3), *heavy), -bound, bound).astype(held_as)


def setup_inputs(seed: int = 0) -> dict:
    key_list = jax.random.split(jax.random.key(seed), 5)
    return {
        "amplitudes": gaussian_with(key_list[0], (CD, IJ), 1.0, 6.0, ((0, 16), (1, 2)), (0, 1, 16, 2.0)),
        "integrals": gaussian_with(key_list[1], (CD, AB), (V * V // 8) ** -0.5, 0.0546875, ((0, 32),), (0, 1, 32, 2.75)),
        "virt_irrep": with_ends(jax.random.randint(key_list[2], (V,), 0, IRREPS), jax.random.fold_in(key_list[2], 1), 0, IRREPS - 1).astype(jnp.int32),
        "occ_irrep": with_ends(jax.random.randint(key_list[3], (O,), 0, IRREPS), jax.random.fold_in(key_list[3], 1), 0, IRREPS - 1).astype(jnp.int32),
    }


def reference(amplitudes, integrals, virt_irrep, occ_irrep):
    column_sym = jnp.bitwise_xor(jnp.repeat(virt_irrep[:A_WIN], V), jnp.tile(virt_irrep, A_WIN))
    row_sym = jnp.bitwise_xor(jnp.repeat(occ_irrep[:I_WIN], O), jnp.tile(occ_irrep, I_WIN))
    amp_blocks = amplitudes.reshape(V, V, I_WIN * O)
    int_blocks = integrals.reshape(V, V, A_WIN * V)

    def step(total, items):
        amp_block, int_block, first_irrep = items
        pair_sym = jnp.bitwise_xor(first_irrep, virt_irrep)
        keep = pair_sym[:, None] == column_sym[None, :]
        kept = int_block * keep.astype(int_block.dtype)
        total = total + jnp.dot(amp_block.astype(jnp.float32).T, kept.astype(jnp.float32),
                                precision=lax.Precision.HIGHEST)
        return total, None

    start = jnp.zeros((I_WIN * O, A_WIN * V), jnp.float32)
    ladder, unused = lax.scan(step, start, (amp_blocks, int_blocks, virt_irrep))
    same = (row_sym[:, None] == column_sym[None, :]).astype(jnp.float32)
    return ladder * same
```

```python
import functools
import math

import jax
import jax.numpy as jnp
from jax import lax
from jax.experimental import pallas as pl
from jax.experimental.pallas import tpu as pltpu
from jax.sharding import PartitionSpec as P

MESH = pl.DeviceIdType.MESH
AMP_SLOTS = 6
INT_SLOTS = 6


def contract_kernel(slabs, amps, virt_count, amp_ref, int_ref, pick_ref, row_sym_ref, col_sym_ref,
                    virt_lanes_ref, virt_ref, out_ref, amp_buf, int_buf, sent, packed,
                    amp_sem, int_sem, send_sem, recv_sem):
    slab = lax.axis_index("slab")
    me = lax.axis_index("amp")
    blocks, cap, block = sent.shape[1], sent.shape[2], sent.shape[3]
    pair_rows = blocks * block
    width = 256

    def amp_copy(step):
        owner = lax.rem(me + 1 + step // blocks, amps)
        start = owner * pair_rows + lax.rem(step, blocks) * block
        slot = lax.rem(step, AMP_SLOTS)
        return pltpu.make_async_copy(
            amp_ref.at[pl.ds(pl.multiple_of(start, 32), block)], amp_buf.at[slot], amp_sem.at[slot])

    def int_copy(step):
        slot = lax.rem(step, INT_SLOTS)
        return pltpu.make_async_copy(
            int_ref.at[pl.ds(pl.multiple_of(step * block, 32), block)], int_buf.at[slot], int_sem.at[slot])

    steps = blocks * amps
    for step in range(min(AMP_SLOTS, steps)):
        amp_copy(jnp.int32(step)).start()
    for step in range(min(INT_SLOTS, blocks)):
        int_copy(jnp.int32(step)).start()

    if amps > 1:
        barrier = pltpu.get_barrier_semaphore()
        for hop in range(1, amps):
            pl.semaphore_signal(barrier, inc=1, device_id=(slab, lax.rem(me + hop, amps)), device_id_type=MESH)
        pl.semaphore_wait(barrier, amps - 1)

    def first_of(owner, index):
        row = (slab * amps + owner) * pair_rows + index * block
        return row // virt_count, lax.rem(row, virt_count)

    def compact(step):
        owner = lax.rem(me + 1 + step // blocks, amps)
        index = lax.rem(step, blocks)
        lead, offset = first_of(owner, index)
        slot = lax.rem(step, AMP_SLOTS)
        amp_copy(step).wait()
        second = virt_lanes_ref[pl.ds(pl.multiple_of(offset, 32), block), :]
        wanted = jnp.bitwise_xor(row_sym_ref[...], virt_ref[lead]).astype(jnp.bfloat16)
        columns = amp_buf.shape[2]
        parts = []
        for begin in range(0, columns, 128):
            end = min(begin + 128, columns)
            piece = amp_buf[slot, :, begin:end]
            parts.append(jnp.where(second[:, : end - begin] == wanted[:, begin:end], piece, jnp.zeros_like(piece)))
        masked = jnp.concatenate(parts, axis=1) if len(parts) > 1 else parts[0]
        return index, lax.dot_general(
            pick_ref[...], masked, (((1,), (1,)), ((), ())), preferred_element_type=jnp.float32
        ).astype(jnp.bfloat16)

    def refill(step):
        @pl.when(step + AMP_SLOTS < steps)
        def _():
            amp_copy(step + AMP_SLOTS).start()

    def remote(hop, index):
        return pltpu.make_async_remote_copy(
            src_ref=sent.at[hop, index],
            dst_ref=packed.at[index, pl.ds(pl.multiple_of(me * cap, 16), cap)],
            send_sem=send_sem.at[hop, index],
            recv_sem=recv_sem.at[hop, index],
            device_id=(slab, lax.rem(me + 1 + hop, amps)),
            device_id_type=MESH)

    def send_step(step, carry):
        index, block_of = compact(step)
        hop = step // blocks
        sent[hop, index] = block_of
        remote(hop, index).start()
        refill(step)
        return carry

    lax.fori_loop(0, steps - blocks, send_step, 0)

    def own_step(step, carry):
        index, block_of = compact(step)
        packed[index, pl.ds(pl.multiple_of(me * cap, 16), cap), :] = block_of
        refill(step)
        return carry

    lax.fori_loop(steps - blocks, steps, own_step, 0)

    out_ref[...] = jnp.zeros_like(out_ref)

    def contract(index, carry):
        slot = lax.rem(index, INT_SLOTS)
        lead, offset = first_of(me, index)
        int_copy(index).wait()
        for hop in range(amps - 1):
            remote(hop, index).wait_recv()
        second = virt_lanes_ref[pl.ds(pl.multiple_of(offset, 32), block), :]
        wanted = jnp.bitwise_xor(col_sym_ref[...], virt_ref[lead]).astype(jnp.bfloat16)
        left = packed[index]
        for begin in range(0, out_ref.shape[1], width):
            parts = []
            for at in range(begin, begin + width, 128):
                piece = int_buf[slot, :, at:at + 128]
                parts.append(jnp.where(second == wanted[:, at:at + 128], piece, jnp.zeros_like(piece)))
            out_ref[:, begin:begin + width] += jnp.dot(
                left, jnp.concatenate(parts, axis=1), preferred_element_type=jnp.float32)

        @pl.when(index + INT_SLOTS < blocks)
        def _():
            int_copy(index + INT_SLOTS).start()
        return carry

    lax.fori_loop(0, blocks, contract, 0)

    def drain(step, carry):
        remote(step // blocks, lax.rem(step, blocks)).wait_send()
        return carry

    lax.fori_loop(0, steps - blocks, drain, 0)


def contract_pairs(amplitudes, integrals, pick, row_sym, col_sym, virt_lanes, virt_irrep):
    slabs = lax.axis_size("slab")
    amps = lax.axis_size("amp")
    cap = pick.shape[0]
    virt_count = virt_irrep.shape[0]
    pair_rows, columns = integrals.shape
    block = math.gcd(pair_rows, virt_count)
    blocks = pair_rows // block
    hops = max(amps - 1, 1)
    vmem = pl.BlockSpec(memory_space=pltpu.VMEM)
    return pl.pallas_call(
        functools.partial(contract_kernel, slabs, amps, virt_count),
        out_shape=jax.ShapeDtypeStruct((amps * cap, columns), jnp.float32),
        in_specs=[pl.BlockSpec(memory_space=pltpu.HBM)] * 2 + [vmem] * 4
        + [pl.BlockSpec(memory_space=pltpu.SMEM)],
        out_specs=vmem,
        scratch_shapes=[
            pltpu.VMEM((AMP_SLOTS, block, amplitudes.shape[1]), jnp.bfloat16),
            pltpu.VMEM((INT_SLOTS, block, columns), jnp.bfloat16),
            pltpu.VMEM((hops, blocks, cap, block), jnp.bfloat16),
            pltpu.VMEM((blocks, amps * cap, block), jnp.bfloat16),
            pltpu.SemaphoreType.DMA((AMP_SLOTS,)),
            pltpu.SemaphoreType.DMA((INT_SLOTS,)),
            pltpu.SemaphoreType.DMA((hops, blocks)),
            pltpu.SemaphoreType.DMA((hops, blocks)),
        ],
        compiler_params=pltpu.CompilerParams(
            collective_id=0, has_side_effects=True, vmem_limit_bytes=56 * 1024 * 1024),
    )(amplitudes, integrals, pick, row_sym, col_sym, virt_lanes, virt_irrep)


def per_device(amplitudes, integrals, virt_irrep, occ_irrep):
    slab_count = lax.axis_size("slab")
    amp_count = lax.axis_size("amp")
    slab_index = lax.axis_index("slab")
    amp_index = lax.axis_index("amp")
    columns = integrals.shape[1]
    pairs_local = amplitudes.shape[1]
    occupied = occ_irrep.shape[0]
    virt_count = virt_irrep.shape[0]
    window_i = pairs_local * amp_count // occupied
    window_a = columns // virt_count
    owned = columns // slab_count
    cap = max(16, pairs_local * 3 // 256 * 16)

    column_sym = jnp.bitwise_xor(
        jnp.repeat(virt_irrep[:window_a], virt_count), jnp.tile(virt_irrep, window_a))
    row_sym_all = jnp.bitwise_xor(
        jnp.repeat(occ_irrep[:window_i], occupied), jnp.tile(occ_irrep, window_i)
    ).reshape(amp_count, pairs_local)
    position = jnp.arange(pairs_local)
    alike = (row_sym_all[:, :, None] == row_sym_all[:, None, :]) & (position[:, None] > position[None, :])
    rank_all = jnp.sum(alike, axis=2, dtype=jnp.int32)
    passes = jnp.max(rank_all) // cap + 1
    row_sym = lax.dynamic_index_in_dim(row_sym_all, amp_index, 0, keepdims=False)
    rank = lax.dynamic_index_in_dim(rank_all, amp_index, 0, keepdims=False)
    owned_sym = lax.dynamic_slice_in_dim(column_sym, slab_index * owned, owned)
    same = row_sym[:, None] == owned_sym[None, :]
    virt_lanes = jnp.broadcast_to(virt_irrep.astype(jnp.bfloat16)[:, None], (virt_count, 128))

    def one_pass(turn, total):
        chosen = rank[None, :] - turn * cap == jnp.arange(cap)[:, None]
        part = contract_pairs(
            amplitudes, integrals, chosen.astype(jnp.bfloat16), row_sym[None, :], column_sym[None, :],
            virt_lanes, virt_irrep)
        part = lax.psum_scatter(part, "amp", scatter_dimension=0, tiled=True)
        part = lax.psum_scatter(part, "slab", scatter_dimension=1, tiled=True)
        spread = lax.dot_general(
            chosen.astype(jnp.float32), part, (((0,), (0,)), ((), ())),
            precision=lax.Precision.HIGHEST, preferred_element_type=jnp.float32)
        return total + jnp.where(same, spread, 0.0)

    return lax.fori_loop(0, passes, one_pass, jnp.zeros((pairs_local, owned), jnp.float32))


def solution(mesh):
    return jax.shard_map(
        per_device,
        mesh=mesh,
        in_specs=(P("slab", "amp"), P(("slab", "amp"), None), P(), P()),
        out_specs=P("amp", "slab"),
        check_vma=False,
    )
```

```python
import functools
import math

import jax
import jax.numpy as jnp
from jax import lax
from jax.experimental import pallas as pl
from jax.experimental.pallas import tpu as pltpu
from jax.sharding import PartitionSpec as P

MESH = pl.DeviceIdType.MESH
AMP_SLOTS = 6
INT_SLOTS = 6


def bit_reversed(index, bits):
    return int(format(index, "b").zfill(bits)[::-1], 2) if bits else 0


def contract_kernel(slabs, amps, virt_count, turned, amp_ref, int_ref, pick_ref, row_sym_ref, col_sym_ref,
                    virt_lanes_ref, virt_row_ref, virt_ref, out_ref, amp_buf, int_buf, sent, packed, acc,
                    halves, arrived, last_in, amp_sem, int_sem, send_sem, recv_sem,
                    half_send, half_recv, last_send, last_recv):
    slab = lax.axis_index("slab")
    me = lax.axis_index("amp")
    blocks, cap, block = sent.shape[1], sent.shape[2], sent.shape[3]
    pair_rows = blocks * block
    width = 256
    bits = slabs.bit_length() - 1
    owned = halves.shape[1]

    def slab_partner(bit):
        return slab + (1 << bit) - 2 * (1 << bit) * lax.rem(slab // (1 << bit), 2)

    def amp_copy(step):
        owner = lax.rem(me + 1 + step // blocks, amps)
        start = owner * pair_rows + lax.rem(step, blocks) * block
        slot = lax.rem(step, AMP_SLOTS)
        if turned:
            source = amp_ref.at[:, pl.ds(pl.multiple_of(start, 128), block)]
        else:
            source = amp_ref.at[pl.ds(pl.multiple_of(start, 32), block)]
        return pltpu.make_async_copy(source, amp_buf.at[slot], amp_sem.at[slot])

    def int_copy(step):
        slot = lax.rem(step, INT_SLOTS)
        return pltpu.make_async_copy(
            int_ref.at[pl.ds(pl.multiple_of(step * block, 32), block)], int_buf.at[slot], int_sem.at[slot])

    steps = blocks * amps
    for step in range(min(AMP_SLOTS, steps)):
        amp_copy(jnp.int32(step)).start()
    for step in range(min(INT_SLOTS, blocks)):
        int_copy(jnp.int32(step)).start()

    barrier = pltpu.get_barrier_semaphore()
    for hop in range(1, amps):
        pl.semaphore_signal(barrier, inc=1, device_id=(slab, lax.rem(me + hop, amps)), device_id_type=MESH)
    for bit in range(bits):
        pl.semaphore_signal(barrier, inc=1, device_id=(slab_partner(bit), me), device_id_type=MESH)
    pl.semaphore_wait(barrier, amps - 1 + bits)

    def first_of(owner, index):
        row = (slab * amps + owner) * pair_rows + index * block
        return row // virt_count, lax.rem(row, virt_count)

    def compact(step):
        owner = lax.rem(me + 1 + step // blocks, amps)
        index = lax.rem(step, blocks)
        lead, offset = first_of(owner, index)
        slot = lax.rem(step, AMP_SLOTS)
        amp_copy(step).wait()
        if turned:
            second = virt_row_ref[:, pl.ds(pl.multiple_of(offset, 128), block)]
            held = jnp.bitwise_xor(second, virt_ref[lead]).astype(jnp.bfloat16)
            parts = []
            for begin in range(0, block, 128):
                piece = amp_buf[slot, :, begin:begin + 128]
                parts.append(jnp.where(row_sym_ref[...] == held[:, begin:begin + 128], piece, jnp.zeros_like(piece)))
            return index, jnp.dot(
                pick_ref[...], jnp.concatenate(parts, axis=1), preferred_element_type=jnp.float32
            ).astype(jnp.bfloat16)
        second = virt_lanes_ref[pl.ds(pl.multiple_of(offset, 32), block), :]
        wanted = jnp.bitwise_xor(row_sym_ref[...], virt_ref[lead]).astype(jnp.bfloat16)
        columns = amp_buf.shape[2]
        parts = []
        for begin in range(0, columns, 128):
            end = min(begin + 128, columns)
            piece = amp_buf[slot, :, begin:end]
            parts.append(jnp.where(second[:, : end - begin] == wanted[:, begin:end], piece, jnp.zeros_like(piece)))
        masked = jnp.concatenate(parts, axis=1) if len(parts) > 1 else parts[0]
        return index, lax.dot_general(
            pick_ref[...], masked, (((1,), (1,)), ((), ())), preferred_element_type=jnp.float32
        ).astype(jnp.bfloat16)

    def refill(step):
        @pl.when(step + AMP_SLOTS < steps)
        def _():
            amp_copy(step + AMP_SLOTS).start()

    def remote(hop, index):
        return pltpu.make_async_remote_copy(
            src_ref=sent.at[hop, index],
            dst_ref=packed.at[index, pl.ds(pl.multiple_of(me * cap, 16), cap)],
            send_sem=send_sem.at[hop, index],
            recv_sem=recv_sem.at[hop, index],
            device_id=(slab, lax.rem(me + 1 + hop, amps)),
            device_id_type=MESH)

    def send_step(step, carry):
        index, block_of = compact(step)
        hop = step // blocks
        sent[hop, index] = block_of
        remote(hop, index).start()
        refill(step)
        return carry

    lax.fori_loop(0, steps - blocks, send_step, 0)

    def own_step(step, carry):
        index, block_of = compact(step)
        packed[index, pl.ds(pl.multiple_of(me * cap, 16), cap), :] = block_of
        refill(step)
        return carry

    lax.fori_loop(steps - blocks, steps, own_step, 0)

    acc[...] = jnp.zeros_like(acc)

    def contract(index, carry):
        slot = lax.rem(index, INT_SLOTS)
        lead, offset = first_of(me, index)
        int_copy(index).wait()
        for hop in range(amps - 1):
            remote(hop, index).wait_recv()
        second = virt_lanes_ref[pl.ds(pl.multiple_of(offset, 32), block), :]
        wanted = jnp.bitwise_xor(col_sym_ref[...], virt_ref[lead]).astype(jnp.bfloat16)
        left = packed[index]
        for begin in range(0, acc.shape[1], width):
            parts = []
            for at in range(begin, begin + width, 128):
                piece = int_buf[slot, :, at:at + 128]
                parts.append(jnp.where(second == wanted[:, at:at + 128], piece, jnp.zeros_like(piece)))
            acc[:, begin:begin + width] += jnp.dot(
                left, jnp.concatenate(parts, axis=1), preferred_element_type=jnp.float32)

        @pl.when(index + INT_SLOTS < blocks)
        def _():
            int_copy(index + INT_SLOTS).start()
        return carry

    lax.fori_loop(0, blocks, contract, 0)

    for owner in range(slabs):
        halves[bit_reversed(owner, bits)] = acc[:, owner * owned:(owner + 1) * owned].T

    base = jnp.int32(0)
    started = []
    filled = 0
    for bit in range(bits):
        count = slabs >> (bit + 1)
        mine = lax.rem(slab // (1 << bit), 2)
        keep = base + mine * count
        leave = base + (1 - mine) * count
        copy = pltpu.make_async_remote_copy(
            src_ref=halves.at[pl.ds(leave, count)],
            dst_ref=arrived.at[pl.ds(filled, count)],
            send_sem=half_send.at[bit],
            recv_sem=half_recv.at[bit],
            device_id=(slab_partner(bit), me),
            device_id_type=MESH)
        copy.start()
        copy.wait_recv()
        started.append(copy)
        halves[pl.ds(keep, count)] = halves[pl.ds(keep, count)] + arrived[filled:filled + count]
        base = keep
        filled += count

    exchanges = []
    for hop in range(amps - 1):
        copy = pltpu.make_async_remote_copy(
            src_ref=halves.at[base],
            dst_ref=last_in.at[hop],
            send_sem=last_send.at[hop],
            recv_sem=last_recv.at[hop],
            device_id=(slab, lax.rem(me + 1 + hop, amps)),
            device_id_type=MESH)
        copy.start()
        exchanges.append(copy)
    total = halves[base]
    for hop, copy in enumerate(exchanges):
        copy.wait_recv()
        total = total + last_in[hop]
    out_ref[...] = total
    for copy in started + exchanges:
        copy.wait_send()

    def drain(step, carry):
        remote(step // blocks, lax.rem(step, blocks)).wait_send()
        return carry

    lax.fori_loop(0, steps - blocks, drain, 0)


def contract_pairs(amplitudes, integrals, pick, row_sym, col_sym, virt_lanes, virt_irrep):
    slabs = lax.axis_size("slab")
    amps = lax.axis_size("amp")
    cap = pick.shape[0]
    virt_count = virt_irrep.shape[0]
    pair_rows, columns = integrals.shape
    block = math.gcd(pair_rows, virt_count)
    blocks = pair_rows // block
    hops = max(amps - 1, 1)
    bits = slabs.bit_length() - 1
    assert slabs == 1 << bits
    owned = columns // slabs
    lanes = amps * cap
    pairs_local = amplitudes.shape[1]
    turned = block % 128 == 0
    if turned:
        amplitudes = amplitudes.T
        row_sym = jnp.broadcast_to(row_sym.astype(jnp.bfloat16).T, (pairs_local, 128))
    vmem = pl.BlockSpec(memory_space=pltpu.VMEM)
    return pl.pallas_call(
        functools.partial(contract_kernel, slabs, amps, virt_count, turned),
        out_shape=jax.ShapeDtypeStruct((owned, lanes), jnp.float32),
        in_specs=[pl.BlockSpec(memory_space=pltpu.HBM)] * 2 + [vmem] * 5
        + [pl.BlockSpec(memory_space=pltpu.SMEM)],
        out_specs=vmem,
        scratch_shapes=[
            pltpu.VMEM((AMP_SLOTS, pairs_local, block) if turned else (AMP_SLOTS, block, pairs_local), jnp.bfloat16),
            pltpu.VMEM((INT_SLOTS, block, columns), jnp.bfloat16),
            pltpu.VMEM((hops, blocks, cap, block), jnp.bfloat16),
            pltpu.VMEM((blocks, lanes, block), jnp.bfloat16),
            pltpu.VMEM((lanes, columns), jnp.float32),
            pltpu.VMEM((slabs, owned, lanes), jnp.float32),
            pltpu.VMEM((max(slabs - 1, 1), owned, lanes), jnp.float32),
            pltpu.VMEM((hops, owned, lanes), jnp.float32),
            pltpu.SemaphoreType.DMA((AMP_SLOTS,)),
            pltpu.SemaphoreType.DMA((INT_SLOTS,)),
            pltpu.SemaphoreType.DMA((hops, blocks)),
            pltpu.SemaphoreType.DMA((hops, blocks)),
            pltpu.SemaphoreType.DMA((max(bits, 1),)),
            pltpu.SemaphoreType.DMA((max(bits, 1),)),
            pltpu.SemaphoreType.DMA((hops,)),
            pltpu.SemaphoreType.DMA((hops,)),
        ],
        compiler_params=pltpu.CompilerParams(
            collective_id=0, has_side_effects=True, vmem_limit_bytes=56 * 1024 * 1024),
    )(amplitudes, integrals, pick, row_sym, col_sym, virt_lanes, virt_irrep[None, :], virt_irrep)


def per_device(amplitudes, integrals, virt_irrep, occ_irrep):
    slab_count = lax.axis_size("slab")
    amp_count = lax.axis_size("amp")
    slab_index = lax.axis_index("slab")
    amp_index = lax.axis_index("amp")
    columns = integrals.shape[1]
    pairs_local = amplitudes.shape[1]
    occupied = occ_irrep.shape[0]
    virt_count = virt_irrep.shape[0]
    window_i = pairs_local * amp_count // occupied
    window_a = columns // virt_count
    owned = columns // slab_count
    cap = max(16, pairs_local * 3 // 256 * 16)

    column_sym = jnp.bitwise_xor(
        jnp.repeat(virt_irrep[:window_a], virt_count), jnp.tile(virt_irrep, window_a))
    row_sym_all = jnp.bitwise_xor(
        jnp.repeat(occ_irrep[:window_i], occupied), jnp.tile(occ_irrep, window_i)
    ).reshape(amp_count, pairs_local)
    position = jnp.arange(pairs_local)
    alike = (row_sym_all[:, :, None] == row_sym_all[:, None, :]) & (position[:, None] > position[None, :])
    rank_all = jnp.sum(alike, axis=2, dtype=jnp.int32)
    passes = jnp.max(rank_all) // cap + 1
    row_sym = lax.dynamic_index_in_dim(row_sym_all, amp_index, 0, keepdims=False)
    rank = lax.dynamic_index_in_dim(rank_all, amp_index, 0, keepdims=False)
    owned_sym = lax.dynamic_slice_in_dim(column_sym, slab_index * owned, owned)
    same = row_sym[:, None] == owned_sym[None, :]
    virt_lanes = jnp.broadcast_to(virt_irrep.astype(jnp.bfloat16)[:, None], (virt_count, 128))

    def one_pass(turn, total):
        chosen = rank[None, :] - turn * cap == jnp.arange(cap)[:, None]
        part = contract_pairs(
            amplitudes, integrals, chosen.astype(jnp.bfloat16), row_sym[None, :], column_sym[None, :],
            virt_lanes, virt_irrep)
        part = lax.dynamic_slice_in_dim(part, amp_index * cap, cap, axis=1)
        spread = lax.dot_general(
            chosen.astype(jnp.float32), part, (((0,), (1,)), ((), ())),
            precision=lax.Precision.HIGHEST, preferred_element_type=jnp.float32)
        return total + jnp.where(same, spread, 0.0)

    return lax.fori_loop(0, passes, one_pass, jnp.zeros((pairs_local, owned), jnp.float32))


def solution(mesh):
    return jax.shard_map(
        per_device,
        mesh=mesh,
        in_specs=(P("slab", "amp"), P(("slab", "amp"), None), P(), P()),
        out_specs=P("amp", "slab"),
        check_vma=False,
    )
```

```python
import functools
import math

import jax
import jax.numpy as jnp
from jax import lax
from jax.experimental import pallas as pl
from jax.experimental.pallas import tpu as pltpu
from jax.sharding import PartitionSpec as P

MESH = pl.DeviceIdType.MESH
AMP_SLOTS = 6
INT_SLOTS = 6


def bit_reversed(index, bits):
    return int(format(index, "b").zfill(bits)[::-1], 2) if bits else 0


def contract_kernel(slabs, amps, virt_count, turned, amp_ref, int_ref, rank_ref, row_sym_ref,
                    virt_row_ref, virt_ref, out_ref, pick_ref, row_lanes_ref, virt_lanes_ref, amp_buf, int_buf, sent, packed, acc,
                    halves, arrived, last_in, amp_sem, int_sem, send_sem, recv_sem,
                    half_send, half_recv, last_send, last_recv):
    slab = lax.axis_index("slab")
    me = lax.axis_index("amp")
    blocks, cap, block = sent.shape[1], sent.shape[2], sent.shape[3]
    pair_rows = blocks * block
    width = 256
    bits = slabs.bit_length() - 1
    owned = halves.shape[1]

    def slab_partner(bit):
        return slab + (1 << bit) - 2 * (1 << bit) * lax.rem(slab // (1 << bit), 2)

    def amp_copy(step):
        owner = lax.rem(me + 1 + step // blocks, amps)
        start = owner * pair_rows + lax.rem(step, blocks) * block
        slot = lax.rem(step, AMP_SLOTS)
        if turned:
            source = amp_ref.at[:, pl.ds(pl.multiple_of(start, 128), block)]
        else:
            source = amp_ref.at[pl.ds(pl.multiple_of(start, 32), block)]
        return pltpu.make_async_copy(source, amp_buf.at[slot], amp_sem.at[slot])

    def int_copy(step):
        slot = lax.rem(step, INT_SLOTS)
        return pltpu.make_async_copy(
            int_ref.at[pl.ds(pl.multiple_of(step * block, 32), block)], int_buf.at[slot], int_sem.at[slot])

    steps = blocks * amps
    for step in range(min(AMP_SLOTS, steps)):
        amp_copy(jnp.int32(step)).start()
    for step in range(min(INT_SLOTS, blocks)):
        int_copy(jnp.int32(step)).start()

    barrier = pltpu.get_barrier_semaphore()
    for hop in range(1, amps):
        pl.semaphore_signal(barrier, inc=1, device_id=(slab, lax.rem(me + hop, amps)), device_id_type=MESH)
    for bit in range(bits):
        pl.semaphore_signal(barrier, inc=1, device_id=(slab_partner(bit), me), device_id_type=MESH)

    slots = lax.broadcasted_iota(jnp.int32, pick_ref.shape, 0)
    pick_ref[...] = jnp.where(slots == rank_ref[...], 1.0, 0.0).astype(jnp.bfloat16)
    row_lanes_ref[...] = jnp.broadcast_to(
        row_sym_ref[...].astype(jnp.float32), (128, row_sym_ref.shape[1])).T.astype(jnp.bfloat16)
    virt_lanes_ref[...] = jnp.broadcast_to(
        virt_row_ref[...].astype(jnp.float32), (128, virt_count)).T.astype(jnp.bfloat16)
    pl.semaphore_wait(barrier, amps - 1 + bits)

    def first_of(owner, index):
        row = (slab * amps + owner) * pair_rows + index * block
        return row // virt_count, lax.rem(row, virt_count)

    def compact(step):
        owner = lax.rem(me + 1 + step // blocks, amps)
        index = lax.rem(step, blocks)
        lead, offset = first_of(owner, index)
        slot = lax.rem(step, AMP_SLOTS)
        amp_copy(step).wait()
        if turned:
            second = virt_row_ref[:, pl.ds(pl.multiple_of(offset, 128), block)]
            held = jnp.bitwise_xor(second, virt_ref[lead]).astype(jnp.bfloat16)
            parts = []
            for begin in range(0, block, 128):
                piece = amp_buf[slot, :, begin:begin + 128]
                parts.append(jnp.where(row_lanes_ref[...] == held[:, begin:begin + 128], piece, jnp.zeros_like(piece)))
            return index, jnp.dot(
                pick_ref[...], jnp.concatenate(parts, axis=1), preferred_element_type=jnp.float32
            ).astype(jnp.bfloat16)
        second = virt_lanes_ref[pl.ds(pl.multiple_of(offset, 32), block), :]
        wanted = jnp.bitwise_xor(row_sym_ref[...], virt_ref[lead]).astype(jnp.bfloat16)
        columns = amp_buf.shape[2]
        parts = []
        for begin in range(0, columns, 128):
            end = min(begin + 128, columns)
            piece = amp_buf[slot, :, begin:end]
            parts.append(jnp.where(second[:, : end - begin] == wanted[:, begin:end], piece, jnp.zeros_like(piece)))
        masked = jnp.concatenate(parts, axis=1) if len(parts) > 1 else parts[0]
        return index, lax.dot_general(
            pick_ref[...], masked, (((1,), (1,)), ((), ())), preferred_element_type=jnp.float32
        ).astype(jnp.bfloat16)

    def refill(step):
        @pl.when(step + AMP_SLOTS < steps)
        def _():
            amp_copy(step + AMP_SLOTS).start()

    def remote(hop, index):
        return pltpu.make_async_remote_copy(
            src_ref=sent.at[hop, index],
            dst_ref=packed.at[index, pl.ds(pl.multiple_of(me * cap, 16), cap)],
            send_sem=send_sem.at[hop, index],
            recv_sem=recv_sem.at[hop, index],
            device_id=(slab, lax.rem(me + 1 + hop, amps)),
            device_id_type=MESH)

    def send_step(step, carry):
        index, block_of = compact(step)
        hop = step // blocks
        sent[hop, index] = block_of
        remote(hop, index).start()
        refill(step)
        return carry

    lax.fori_loop(0, steps - blocks, send_step, 0)

    def own_step(step, carry):
        index, block_of = compact(step)
        packed[index, pl.ds(pl.multiple_of(me * cap, 16), cap), :] = block_of
        refill(step)
        return carry

    lax.fori_loop(steps - blocks, steps, own_step, 0)

    acc[...] = jnp.zeros_like(acc)

    def contract(index, carry):
        slot = lax.rem(index, INT_SLOTS)
        lead, offset = first_of(me, index)
        int_copy(index).wait()
        for hop in range(amps - 1):
            remote(hop, index).wait_recv()
        second = virt_lanes_ref[pl.ds(pl.multiple_of(offset, 32), block), :]
        by_first = [
            jnp.bitwise_xor(virt_row_ref[...], jnp.bitwise_xor(virt_ref[first], virt_ref[lead])).astype(jnp.bfloat16)
            for first in range(acc.shape[1] // virt_count)]
        wanted = jnp.concatenate(by_first, axis=1)
        left = packed[index]
        for begin in range(0, acc.shape[1], width):
            parts = []
            for at in range(begin, begin + width, 128):
                piece = int_buf[slot, :, at:at + 128]
                parts.append(jnp.where(second == wanted[:, at:at + 128], piece, jnp.zeros_like(piece)))
            acc[:, begin:begin + width] += jnp.dot(
                left, jnp.concatenate(parts, axis=1), preferred_element_type=jnp.float32)

        @pl.when(index + INT_SLOTS < blocks)
        def _():
            int_copy(index + INT_SLOTS).start()
        return carry

    lax.fori_loop(0, blocks, contract, 0)

    for owner in range(slabs):
        halves[bit_reversed(owner, bits)] = acc[:, owner * owned:(owner + 1) * owned].T

    base = jnp.int32(0)
    started = []
    filled = 0
    for bit in range(bits):
        count = slabs >> (bit + 1)
        mine = lax.rem(slab // (1 << bit), 2)
        keep = base + mine * count
        leave = base + (1 - mine) * count
        copy = pltpu.make_async_remote_copy(
            src_ref=halves.at[pl.ds(leave, count)],
            dst_ref=arrived.at[pl.ds(filled, count)],
            send_sem=half_send.at[bit],
            recv_sem=half_recv.at[bit],
            device_id=(slab_partner(bit), me),
            device_id_type=MESH)
        copy.start()
        copy.wait_recv()
        started.append(copy)
        halves[pl.ds(keep, count)] = halves[pl.ds(keep, count)] + arrived[filled:filled + count]
        base = keep
        filled += count

    exchanges = []
    for hop in range(amps - 1):
        copy = pltpu.make_async_remote_copy(
            src_ref=halves.at[base],
            dst_ref=last_in.at[hop],
            send_sem=last_send.at[hop],
            recv_sem=last_recv.at[hop],
            device_id=(slab, lax.rem(me + 1 + hop, amps)),
            device_id_type=MESH)
        copy.start()
        exchanges.append(copy)
    total = halves[base]
    for hop, copy in enumerate(exchanges):
        copy.wait_recv()
        total = total + last_in[hop]
    out_ref[...] = total
    for copy in started + exchanges:
        copy.wait_send()

    def drain(step, carry):
        remote(step // blocks, lax.rem(step, blocks)).wait_send()
        return carry

    lax.fori_loop(0, steps - blocks, drain, 0)


def contract_pairs(amplitudes, integrals, rank, cap, row_sym, virt_irrep):
    slabs = lax.axis_size("slab")
    amps = lax.axis_size("amp")
    virt_count = virt_irrep.shape[0]
    pair_rows, columns = integrals.shape
    block = math.gcd(pair_rows, virt_count)
    blocks = pair_rows // block
    hops = max(amps - 1, 1)
    bits = slabs.bit_length() - 1
    assert slabs == 1 << bits
    owned = columns // slabs
    lanes = amps * cap
    pairs_local = amplitudes.shape[1]
    turned = block % 128 == 0
    if turned:
        amplitudes = amplitudes.T
    vmem = pl.BlockSpec(memory_space=pltpu.VMEM)
    return pl.pallas_call(
        functools.partial(contract_kernel, slabs, amps, virt_count, turned),
        out_shape=jax.ShapeDtypeStruct((owned, lanes), jnp.float32),
        in_specs=[pl.BlockSpec(memory_space=pltpu.HBM)] * 2 + [vmem] * 3
        + [pl.BlockSpec(memory_space=pltpu.SMEM)],
        out_specs=vmem,
        scratch_shapes=[
            pltpu.VMEM((cap, pairs_local), jnp.bfloat16),
            pltpu.VMEM((pairs_local, 128), jnp.bfloat16),
            pltpu.VMEM((virt_count, 128), jnp.bfloat16),
            pltpu.VMEM((AMP_SLOTS, pairs_local, block) if turned else (AMP_SLOTS, block, pairs_local), jnp.bfloat16),
            pltpu.VMEM((INT_SLOTS, block, columns), jnp.bfloat16),
            pltpu.VMEM((hops, blocks, cap, block), jnp.bfloat16),
            pltpu.VMEM((blocks, lanes, block), jnp.bfloat16),
            pltpu.VMEM((lanes, columns), jnp.float32),
            pltpu.VMEM((slabs, owned, lanes), jnp.float32),
            pltpu.VMEM((max(slabs - 1, 1), owned, lanes), jnp.float32),
            pltpu.VMEM((hops, owned, lanes), jnp.float32),
            pltpu.SemaphoreType.DMA((AMP_SLOTS,)),
            pltpu.SemaphoreType.DMA((INT_SLOTS,)),
            pltpu.SemaphoreType.DMA((hops, blocks)),
            pltpu.SemaphoreType.DMA((hops, blocks)),
            pltpu.SemaphoreType.DMA((max(bits, 1),)),
            pltpu.SemaphoreType.DMA((max(bits, 1),)),
            pltpu.SemaphoreType.DMA((hops,)),
            pltpu.SemaphoreType.DMA((hops,)),
        ],
        compiler_params=pltpu.CompilerParams(
            collective_id=0, has_side_effects=True, vmem_limit_bytes=56 * 1024 * 1024),
    )(amplitudes, integrals, rank, row_sym, virt_irrep[None, :], virt_irrep)


def per_device(amplitudes, integrals, virt_irrep, occ_irrep):
    slab_count = lax.axis_size("slab")
    amp_count = lax.axis_size("amp")
    slab_index = lax.axis_index("slab")
    amp_index = lax.axis_index("amp")
    columns = integrals.shape[1]
    pairs_local = amplitudes.shape[1]
    occupied = occ_irrep.shape[0]
    virt_count = virt_irrep.shape[0]
    window_i = pairs_local * amp_count // occupied
    window_a = columns // virt_count
    owned = columns // slab_count
    cap = max(16, pairs_local * 3 // 256 * 16)

    column_sym = jnp.bitwise_xor(
        jnp.repeat(virt_irrep[:window_a], virt_count), jnp.tile(virt_irrep, window_a))
    row_sym_all = jnp.bitwise_xor(
        jnp.repeat(occ_irrep[:window_i], occupied), jnp.tile(occ_irrep, window_i)
    ).reshape(amp_count, pairs_local)
    position = jnp.arange(pairs_local)
    alike = (row_sym_all[:, :, None] == row_sym_all[:, None, :]) & (position[:, None] > position[None, :])
    rank_all = jnp.sum(alike, axis=2, dtype=jnp.int32)
    passes = jnp.max(rank_all) // cap + 1
    row_sym = lax.dynamic_index_in_dim(row_sym_all, amp_index, 0, keepdims=False)
    rank = lax.dynamic_index_in_dim(rank_all, amp_index, 0, keepdims=False)
    owned_sym = lax.dynamic_slice_in_dim(column_sym, slab_index * owned, owned)
    same = row_sym[:, None] == owned_sym[None, :]

    def one_pass(turn, total):
        chosen = rank[None, :] - turn * cap == jnp.arange(cap)[:, None]
        part = contract_pairs(
            amplitudes, integrals, rank[None, :] - turn * cap, cap, row_sym[None, :], virt_irrep)
        part = lax.dynamic_slice_in_dim(part, amp_index * cap, cap, axis=1)
        spread = lax.dot_general(
            chosen.astype(jnp.float32), part, (((0,), (1,)), ((), ())),
            precision=lax.Precision.HIGHEST, preferred_element_type=jnp.float32)
        return total + jnp.where(same, spread, 0.0)

    return lax.fori_loop(0, passes, one_pass, jnp.zeros((pairs_local, owned), jnp.float32))


def solution(mesh):
    return jax.shard_map(
        per_device,
        mesh=mesh,
        in_specs=(P("slab", "amp"), P(("slab", "amp"), None), P(), P()),
        out_specs=P("amp", "slab"),
        check_vma=False,
    )
```
